32 devices in a mesh: fsdp: 8 (over z, x), ckpt: 4 (over y, core).
Axes of the slice: x: 2, y: 2, z: 4, core: 2. Of those that a mesh axis runs over, the one named last changes fastest.
Arguments:
- act_table: bfloat16 [4, 2048, 4096], P('ckpt', 'fsdp'), may hold values from -6 to 6
- token_ids: int32 [4, 2048], P('ckpt'), may hold values from 0 to 2047, each once within a row
- lengths: int32 [4, 8], P('ckpt'), may hold values from 1 to 384, 2048 in all within a row
- grads: bfloat16 [4, 2048, 14336], P('ckpt', 'fsdp'), may hold values from -0.19921875 to 0.19921875
- weights: bfloat16 [4, 8, 4096, 1792], P('ckpt', 'fsdp'), may hold values from -6 to 6
Outputs:
- merged: bfloat16 [8, 4096, 1792], P('fsdp', 'ckpt')
- merge_weight: float32 [8, 4096, 1792], P('fsdp', 'ckpt')
The draws below stay inside these ranges and needn't reach their ends.
Inputs may be any that keep to these rules, and one draw needn't show every extreme that they name: `token_ids`: each checkpoint's row names every row of the activation table once. One checkpoint's lengths sum to 2048, and one of them is exactly 384.
All inputs are finite; a program needn't handle non-finite values.
Results may differ from the reference program's by a relative error of at most 0.001.
Values may be sent and summed in bfloat16 or wider, within the bound.
No kernel may reach another device: no remote copies, remote signals or barrier semaphores. Data moves between devices by JAX's collectives and lax.ppermute only.
A program may use at most 256 MiB of HBM per device.

```python
import math
import jax
import jax.numpy as jnp
import numpy as np
from jax import lax

D = 4096
FFW = 14336
NCB = 8
EX = 8
CKPTS = 4
NFB = 1
TILES = 8
TOK = 2048
MOST = 384
N_CKPT = 4


def levels(stream_key, extent, pieces, low, top_value):
    level = 1.0
    for dim, blocks in pieces:
        heights = jax.random.uniform(jax.random.fold_in(jax.random.fold_in(stream_key, 6), dim), (blocks,), jnp.float32, low / len(pieces), top_value / len(pieces))
        level = level * jnp.repeat(jnp.exp(heights), extent[dim] // blocks).reshape((-1,) + (1,) * (len(extent) - 1 - dim))
    return level


def split_up(number_of, total, reach, slope):
    weights = [(1 << 20) // math.isqrt(standing ** slope) + 1 for standing in range(2, number_of + 1)]
    rest, holding = total - reach - (number_of - 1), [1] * (number_of - 1)
    while rest > 0:
        movable = [i for i in range(number_of - 1) if holding[i] < reach]
        pool, remaining = sum([weights[i] for i in movable]), rest
        for i in movable:
            addition = min(reach - holding[i], max(1, remaining * weights[i] // pool), rest)
            holding[i] = holding[i] + addition
            rest = rest - addition
    return np.array([reach] + holding)


def ragged_sizes(own_key, number_of, total, most, lean):
    if number_of == 2:
        one = jax.random.randint(own_key, (), max(1, total - most), min(most, total - 1) + 1)
        return jnp.stack([one, total - one])
    sizes = jnp.asarray(split_up(number_of, total, most, lean), jnp.int32)
    twos = (number_of - 1) // 2
    giver, sink = sizes[1:1 + 2 * twos:2], sizes[2:2 + 2 * twos:2]
    margin = jnp.minimum(giver - 1, most - sink)
    shifted = jax.random.randint(jax.random.fold_in(own_key, 1), (twos,), 0, 1 << 20) % (margin + 1)
    sizes = sizes.at[1:1 + 2 * twos:2].set(giver - shifted).at[2:2 + 2 * twos:2].set(sink + shifted)
    return sizes[jax.random.permutation(jax.random.fold_in(own_key, 2), number_of)]


def bell_draw(stream_key, dims, deviation, reach, cuts=(), kind=jnp.bfloat16):
    level = levels(stream_key, dims, cuts, -0.22, 0.18) if cuts else 1.0
    result = jax.random.normal(stream_key, dims, jnp.float32) * deviation * level
    return jnp.minimum(jnp.maximum(result, -reach), reach).astype(kind)


def setup_inputs(seed: int = 0) -> dict:
    seeds = jax.random.split(jax.random.key(seed), 6)
    return {
        "act_table": bell_draw(seeds[0], (CKPTS, TOK, D), 1.0, 6.0, ((0, 4), (1, 8))),
        "token_ids": jax.vmap(lambda own: jax.random.permutation(own, TOK))(jax.random.split(seeds[1], CKPTS)).reshape((CKPTS, TOK)).astype(jnp.int32),
        "lengths": jax.vmap(lambda own: ragged_sizes(own, EX, TOK, MOST, 1))(jax.random.split(seeds[2], CKPTS)).reshape((CKPTS, EX)).astype(jnp.int32),
        "grads": bell_draw(seeds[3], (CKPTS, TOK, FFW), 0.03, 0.19921875, ((0, 4), (1, 8))),
        "weights": bell_draw(seeds[4], (CKPTS, TILES, D // NFB, FFW // NCB), 1.0, 6.0, ((0, 4), (1, 8))),
    }


prior_mass = 0.1


def example_fisher(act_rows, grad_rows, example_lengths):
    row_starts = (jnp.cumsum(example_lengths) - example_lengths).astype(jnp.int32)
    padded_rows = jnp.concatenate([act_rows, jnp.zeros((MOST, act_rows.shape[1]), act_rows.dtype)], 0)
    padded_grads = jnp.concatenate([grad_rows, jnp.zeros((MOST, grad_rows.shape[1]), grad_rows.dtype)], 0)
    positions = jnp.arange(MOST, dtype=jnp.int32)

    def add_example(example, running):
        row_start = row_starts[example].astype(jnp.int32)
        act_block = lax.dynamic_slice_in_dim(padded_rows, row_start, MOST, 0)
        keep = (positions < example_lengths[example])[:, None]
        act_block = jnp.where(keep, act_block, jnp.zeros_like(act_block))
        grad_block = lax.dynamic_slice_in_dim(padded_grads, row_start, MOST, 0)
        example_grad = lax.dot_general(act_block, grad_block, (((0,), (0,)), ((), ())), preferred_element_type=jnp.float32)
        return running + example_grad * example_grad

    start_value = jnp.zeros((act_rows.shape[1], grad_rows.shape[1]), jnp.float32)
    return lax.fori_loop(0, example_lengths.shape[0], add_example, start_value)


def to_tiles(full):
    blocked = full.reshape(NFB, D // NFB, NCB, FFW // NCB)
    return jnp.transpose(blocked, (0, 2, 1, 3)).reshape(NFB * NCB, D // NFB, FFW // NCB)


def reference(act_table, token_ids, lengths, grads, weights):
    numerator = jnp.zeros((TILES, D // NFB, FFW // NCB), jnp.float32)
    denominator = jnp.zeros((TILES, D // NFB, FFW // NCB), jnp.float32)
    for member in range(N_CKPT):
        act_rows = act_table[member][token_ids[member]]
        fisher = to_tiles(example_fisher(act_rows, grads[member], lengths[member]))
        fisher_mass = fisher + prior_mass
        numerator = numerator + fisher_mass * weights[member].astype(jnp.float32)
        denominator = denominator + fisher_mass
    return (numerator / denominator).astype(jnp.bfloat16), denominator / N_CKPT
```

```python
import functools

import jax
import jax.numpy as jnp
from jax import lax
from jax.experimental import pallas as pl
from jax.experimental.pallas import tpu as pltpu
from jax.sharding import PartitionSpec as P

NCB = 8
MOST = 384
LANES = 128

prior_mass = 0.1


def swap(value, axis, bit):
    size = lax.axis_size(axis)
    return lax.ppermute(value, axis, [(i, i ^ bit) for i in range(size)])


def shift(value, axis, step):
    size = lax.axis_size(axis)
    pairs = [(i, i + step) for i in range(size) if 0 <= i + step < size]
    return lax.ppermute(value, axis, pairs)


def slot_kernel(first, last, group_size, window, bounds, act, grad, weight, *refs):
    if first:
        outs = refs[:-1]
    else:
        prev_den, prev_num = refs[:2]
        outs = refs[2:-1]
    mass = refs[-1]
    tokens = grad.shape[0]
    count = bounds.shape[1]
    mass[...] = jnp.full(mass.shape, prior_mass, jnp.float32)

    def add_example(example, carry):
        begin = bounds[0, example]
        end = begin + bounds[1, example]
        base = jnp.minimum((begin // LANES) * LANES, tokens - window)
        base = pl.multiple_of(base, LANES)
        place = base + lax.broadcasted_iota(jnp.int32, (window, grad.shape[1]), 0)
        rows = grad[pl.ds(base, window), :]
        rows = jnp.where((place >= begin) & (place < end), rows, jnp.zeros_like(rows))
        one = jnp.dot(act[:, pl.ds(base, window)], rows, preferred_element_type=jnp.float32)
        mass[...] += one * one
        return carry

    lax.fori_loop(0, count, add_example, 0)
    den = mass[...]
    num = den * weight[...].astype(jnp.float32)
    if not first:
        den = den + prev_den[...]
        num = num + prev_num[...]
    if last:
        outs[0][...] = (num / den).astype(jnp.bfloat16)
        outs[1][...] = den / group_size
    else:
        outs[0][...] = den
        outs[1][...] = num


def add_slot(bounds, act, grad, weight, prev, last, group_size):
    features, tokens = act.shape
    width = grad.shape[1]
    block = 256 if width % 256 == 0 else LANES
    window = min(-(-(MOST + LANES - 1) // LANES) * LANES, tokens)
    first = prev is None
    col = lambda j, b: (0, j)
    tile = pl.BlockSpec((features, block), col)
    in_specs = [
        pl.BlockSpec((features, tokens), lambda j, b: (0, 0), pipeline_mode=pl.Buffered(1)),
        pl.BlockSpec((tokens, block), col),
        tile,
    ]
    operands = [act, grad, weight]
    if not first:
        in_specs += [tile, tile]
        operands += list(prev)
    shape = (features, width)
    if last:
        outs = (jax.ShapeDtypeStruct(shape, jnp.bfloat16), jax.ShapeDtypeStruct(shape, jnp.float32))
    else:
        outs = (jax.ShapeDtypeStruct(shape, jnp.float32), jax.ShapeDtypeStruct(shape, jnp.float32))
    return pl.pallas_call(
        functools.partial(slot_kernel, first, last, group_size, window),
        out_shape=outs,
        grid_spec=pltpu.PrefetchScalarGridSpec(
            num_scalar_prefetch=1,
            grid=(width // block,),
            in_specs=in_specs,
            out_specs=(tile, tile),
            scratch_shapes=[pltpu.VMEM((features, block), jnp.float32)],
        ),
        cost_estimate=pl.CostEstimate(
            flops=2 * bounds.shape[1] * window * features * width,
            bytes_accessed=2 * (features + width) * tokens + 18 * features * width,
            transcendentals=0,
        ),
    )(bounds, *operands)


def gather_line(own):
    n = lax.axis_size("fsdp") // 2
    z = lax.axis_index("fsdp") // 2
    right, left = [own], [own]
    for k in range(1, n):
        right.append(shift(right[-1], "fsdp", 2))
        left.append(shift(left[-1], "fsdp", -2))
    chunks = []
    for k in range(n):
        got = own if k == 0 else jnp.where(z >= k, right[k], left[n - k])
        chunks += [got, swap(got, "fsdp", 1)]
    return chunks


def place_of(ids, local):
    n = lax.axis_size("fsdp") // 2
    me = lax.axis_index("fsdp")
    source = ids // local
    k = (me // 2 - source // 2) % n
    s = (source % 2) ^ (me % 2)
    return (2 * k + s) * local + ids % local


def permuted(rows, place):
    hot = (lax.broadcasted_iota(jnp.int32, (rows.shape[0], place.shape[0]), 0) == place[None, :])
    return lax.dot_general(
        rows, hot.astype(rows.dtype), (((0,), (0,)), ((), ())), preferred_element_type=jnp.float32
    ).astype(rows.dtype)


def body(act_table, token_ids, lengths, grads, weights):
    group = lax.axis_size("fsdp")
    size = lax.axis_size("ckpt")
    c = lax.axis_index("ckpt")
    y, core = c // 2, c % 2
    row_blocks = group // NCB
    own_rows, own_grads, own_weight = act_table[0], grads[0], weights[0, 0]
    local, depth = own_rows.shape
    tokens = token_ids.shape[1]
    features = depth // row_blocks // size

    starts = jnp.cumsum(lengths[0]) - lengths[0]
    meta = jnp.concatenate([starts, lengths[0], token_ids[0]]).astype(jnp.int32)
    metas = [meta, swap(meta, "ckpt", 1), swap(meta, "ckpt", 2), swap(meta, "ckpt", 3)]
    count = lengths.shape[1]

    parts = own_rows.reshape(local, row_blocks, size, features)
    half = 2
    def quarter(value, index):
        return lax.dynamic_index_in_dim(value, index, 2, keepdims=False)
    far = lax.dynamic_slice_in_dim(parts, (1 - y) * half, half, 2)
    far = swap(far, "ckpt", 2)
    near = lax.dynamic_slice_in_dim(parts, y * half, half, 2)
    act0, act2 = quarter(near, core), quarter(far, core)
    act1 = swap(quarter(near, 1 - core), "ckpt", 1)
    act3 = swap(quarter(far, 1 - core), "ckpt", 1)

    width = own_grads.shape[1] // NCB
    grad_parts = jnp.transpose(own_grads.reshape(local, NCB, width), (1, 0, 2))
    if row_blocks > 1:
        grad_parts = jnp.broadcast_to(grad_parts[None], (row_blocks, NCB, local, width))
        grad_parts = grad_parts.reshape(group, local, width)
    grad0 = lax.all_to_all(grad_parts, "fsdp", split_axis=0, concat_axis=0, tiled=True)
    grad0 = grad0.reshape(tokens, width)
    grad2 = swap(grad0, "ckpt", 2)
    grad1 = swap(grad0, "ckpt", 1)
    grad3 = swap(grad2, "ckpt", 1)

    far_w = lax.dynamic_slice_in_dim(own_weight, (1 - y) * 2 * features, 2 * features, 0)
    far_w = swap(far_w, "ckpt", 2)
    def rows_of(value, index):
        return lax.dynamic_slice_in_dim(value, index * features, features, 0)
    weight0 = rows_of(own_weight, c)
    weight1 = swap(rows_of(own_weight, y * 2 + 1 - core), "ckpt", 1)
    weight2 = rows_of(far_w, core)
    weight3 = swap(rows_of(far_w, 1 - core), "ckpt", 1)

    def gathered(a, b):
        if row_blocks == 1:
            pair = jnp.stack([a[:, 0], b[:, 0]])
            table = jnp.concatenate(gather_line(pair), axis=1)
            return table[0], table[1]
        both = jnp.stack([a, b])
        both = jnp.transpose(both, (2, 0, 1, 3))[:, None]
        both = jnp.broadcast_to(both, (row_blocks, NCB, 2, local, features))
        both = both.reshape(group, 2, local, features)
        table = lax.all_to_all(both, "fsdp", split_axis=0, concat_axis=0, tiled=True)
        return table[:, 0].reshape(tokens, features), table[:, 1].reshape(tokens, features)

    tables = gathered(act0, act1) + gathered(act2, act3)
    grad_slots = (grad0, grad1, grad2, grad3)
    weight_slots = (weight0, weight1, weight2, weight3)
    carry = None
    for j in range(size):
        ids = metas[j][2 * count:]
        place = place_of(ids, local) if row_blocks == 1 else ids
        act = permuted(tables[j], place)
        bounds = metas[j][:2 * count].reshape(2, count)
        carry = add_slot(bounds, act, grad_slots[j], weight_slots[j], carry, j == size - 1, size)
    merged, merge_weight = carry
    return merged[None], merge_weight[None]


def solution(mesh):
    placed = (
        P("ckpt", "fsdp", None),
        P("ckpt", None),
        P("ckpt", None),
        P("ckpt", "fsdp", None),
        P("ckpt", "fsdp", None, None),
    )
    return jax.shard_map(
        body,
        mesh=mesh,
        in_specs=placed,
        out_specs=(P("fsdp", "ckpt", None), P("fsdp", "ckpt", None)),
        check_vma=False,
    )
```

```python
import functools

import jax
import jax.numpy as jnp
from jax import lax
from jax.experimental import pallas as pl
from jax.experimental.pallas import tpu as pltpu
from jax.sharding import PartitionSpec as P


NCB = 8
MOST = 384
LANES = 128
COLS = (256, 128)
ROWS = 256
CUT = 512

prior_mass = 0.1


def swap(value, axis, bit):
    size = lax.axis_size(axis)
    return lax.ppermute(value, axis, [(i, i ^ bit) for i in range(size)])


def slot_kernel(slots, first, last, group_size, window, block, bounds, act, *refs):
    grads, refs = refs[:slots], refs[slots:]
    weights, refs = refs[:slots], refs[slots:]
    den, num = refs[-2:]
    outs, prev = refs[-4:-2], refs[:-4]
    (_, features, tokens), count = act.shape, (bounds.shape[1] - 1) // 2
    step = ROWS if features % ROWS == 0 else features

    def base_of(slot, example):
        base = jnp.minimum((bounds[slot, example] // LANES) * LANES, tokens - window)
        return pl.multiple_of(base, LANES)

    for slot in range(slots):
        examples = []
        for example in range(count):
            begin = bounds[slot, example]
            end = begin + bounds[slot, count + example]
            base = base_of(slot, example)
            place = base + lax.broadcasted_iota(jnp.int32, (window, block), 0)
            rows = grads[slot][pl.ds(base, window), :]
            rows = jnp.where((place >= begin) & (place < end), rows, jnp.zeros_like(rows))
            examples.append((base, rows))
        for low in range(0, features, step):
            part = pl.ds(low, step)
            total = jnp.float32(prior_mass)
            for base, rows in examples:
                mine = act[slot, part, pl.ds(base, window)]
                one = jnp.dot(mine, rows, preferred_element_type=jnp.float32)
                total = total + one * one
            weighted = total * weights[slot][part, :].astype(jnp.float32)
            if slot > 0:
                total, weighted = total + den[part, :], weighted + num[part, :]
            elif not first:
                total, weighted = total + prev[0][part, :], weighted + prev[1][part, :]
            den[part, :] = total
            num[part, :] = weighted

    if last:
        outs[0][...] = (num[...] / den[...]).astype(jnp.bfloat16)
        outs[1][...] = den[...] / group_size
    else:
        outs[0][...] = den[...]
        outs[1][...] = num[...]


def add_slots(bounds, act, at, grads, weights, prev, done, offset, last, group_size):
    slots = len(grads)
    (_, features, tokens), count = act.shape, (bounds.shape[1] - 1) // 2
    span, width = grads[0].shape[1], weights[0].shape[1]
    block = next(b for b in COLS if span % b == 0 and offset % b == 0)
    window = min(-(-(MOST + LANES - 1) // LANES) * LANES, tokens)
    first = prev is None
    skip = offset // block
    chunk = pl.BlockSpec((features, block), lambda j, b: (0, j))
    tile = pl.BlockSpec((features, block), lambda j, b: (0, j + skip))
    whole = pl.BlockSpec(
        (slots, features, tokens), lambda j, b: (at // slots, 0, 0), pipeline_mode=pl.Buffered(1)
    )
    in_specs = [whole]
    in_specs += [pl.BlockSpec((tokens, block), lambda j, b: (0, j))] * slots
    in_specs += [
        pl.BlockSpec((features, block), lambda j, b, s=s: (b[s, 2 * count], j + skip))
        for s in range(slots)
    ]
    operands = [act] + list(grads) + list(weights)
    if not first:
        in_specs += [chunk, chunk]
        operands += list(prev)
    aliases = {}
    if last:
        outs = (
            jax.ShapeDtypeStruct((features, width), jnp.bfloat16),
            jax.ShapeDtypeStruct((features, width), jnp.float32),
        )
        if done is not None:
            aliases = {len(operands) + 1: 0, len(operands) + 2: 1}
            in_specs += [pl.BlockSpec(memory_space=pl.ANY)] * 2
            operands += list(done)
    else:
        outs = (jax.ShapeDtypeStruct((features, span), jnp.float32),) * 2
    return pl.pallas_call(
        functools.partial(slot_kernel, slots, first, last, group_size, window, block),
        out_shape=outs,
        grid_spec=pltpu.PrefetchScalarGridSpec(
            num_scalar_prefetch=1,
            grid=(span // block,),
            in_specs=in_specs,
            out_specs=(tile, tile) if last else (chunk, chunk),
            scratch_shapes=[
                pltpu.VMEM((features, block), jnp.float32),
                pltpu.VMEM((features, block), jnp.float32),
            ],
        ),
        input_output_aliases=aliases,
        cost_estimate=pl.CostEstimate(
            flops=slots * 2 * count * window * features * span,
            bytes_accessed=slots * 2 * (features + span) * tokens + 18 * features * span,
            transcendentals=0,
        ),
    )(bounds, *operands)


def gather_line(own):
    size = lax.axis_size("fsdp")
    n = size // 2

    def send(value, pairs):
        return lax.ppermute(value, "fsdp", pairs)

    line = range(size)
    right, left = [own], [own]
    pair_right = [send(own, [(i, i ^ 1) for i in line])]
    pair_left = [pair_right[0]]
    for k in range(1, n):
        reach = [i for i in line if i // 2 >= k - 1 and i // 2 + 1 < n]
        right.append(send(right[-1], [(i, i + 2) for i in reach]))
        reach = [i for i in line if i // 2 < n - k + 1 and i // 2 >= 1]
        left.append(send(left[-1], [(i, i - 2) for i in reach]))
        pair_right.append(send(right[-1], [(i, i ^ 1) for i in line if i // 2 >= k]))
        pair_left.append(send(left[-1], [(i, i ^ 1) for i in line if i // 2 < n - k]))
    return right, left, pair_right, pair_left


def permute_kernel(n, where, ids, *refs):
    sources, (out, table, sems) = refs[:-3], refs[-3:]
    right, left = sources[:n], sources[n:2 * n - 1]
    pair_right, pair_left = sources[2 * n - 1:3 * n - 1], sources[3 * n - 1:]
    slot, step = pl.program_id(0), pl.program_id(1)
    z, x = where[0], where[1]

    def place(k, s):
        return lax.rem(z - k + n, n) * 2 + (x if s == 0 else 1 - x)

    def copy(source, part, k, s):
        return pltpu.make_async_copy(source.at[part], table.at[part, place(k, s)], sems.at[part, k, s])

    @pl.when((slot == 0) & (step == 0))
    def _():
        for part in range(2):
            for s, ups, downs in ((0, right, left), (1, pair_right, pair_left)):
                copy(ups[0], part, 0, s).start()
                for k in range(1, n):
                    @pl.when(z >= k)
                    def _():
                        copy(ups[k], part, k, s).start()

                    @pl.when(z < k)
                    def _():
                        copy(downs[n - k - 1], part, k, s).start()

    for part in range(2):
        @pl.when((slot == part) & (step == 0))
        def _():
            for k in range(n):
                for s in range(2):
                    copy(right[0], part, k, s).wait()

    rows = table[slot].reshape(-1, table.shape[-1])
    width = min(ROWS, ids.shape[1])
    for low in range(0, ids.shape[1], width):
        mine = ids[0, low:low + width]
        hot = lax.broadcasted_iota(jnp.int32, (width, rows.shape[0]), 1) == mine
        hot = jnp.where(hot, jnp.float32(1), jnp.float32(0)).astype(rows.dtype)
        picked = jnp.dot(hot, rows, preferred_element_type=jnp.float32).astype(rows.dtype)
        out[0, :, low:low + width] = picked.T


def permute_pair(ids, pieces):
    right, left, pair_right, pair_left = pieces
    n = len(right)
    _, local, features = right[0].shape
    tokens = ids.shape[1]
    rows = min(2 * ROWS, tokens)
    me = lax.axis_index("fsdp")
    where = jnp.stack([me // 2, me % 2]).astype(jnp.int32)
    operands = [*right, *left[1:], *pair_right, *pair_left[1:]]
    return pl.pallas_call(
        functools.partial(permute_kernel, n),
        out_shape=jax.ShapeDtypeStruct((2, features, tokens), right[0].dtype),
        grid_spec=pltpu.PrefetchScalarGridSpec(
            num_scalar_prefetch=1,
            grid=(2, tokens // rows),
            in_specs=[pl.BlockSpec((1, rows, 1), lambda p, t, w: (p, t, 0))]
            + [pl.BlockSpec(memory_space=pl.ANY)] * len(operands),
            out_specs=pl.BlockSpec((1, features, rows), lambda p, t, w: (p, 0, t)),
            scratch_shapes=[
                pltpu.VMEM((2, 2 * n, local, features), right[0].dtype),
                pltpu.SemaphoreType.DMA((2, n, 2)),
            ],
        ),
        cost_estimate=pl.CostEstimate(
            flops=4 * tokens * tokens * features, bytes_accessed=8 * tokens * features, transcendentals=0
        ),
    )(where, ids[:, :, None], *operands)


def permuted(rows, place):
    hot = (lax.broadcasted_iota(jnp.int32, (rows.shape[0], place.shape[0]), 0) == place[None, :])
    return lax.dot_general(
        rows, hot.astype(rows.dtype), (((0,), (0,)), ((), ())), preferred_element_type=jnp.float32
    ).astype(rows.dtype)


def body(act_table, token_ids, lengths, grads, weights):
    group = lax.axis_size("fsdp")
    size = lax.axis_size("ckpt")
    c = lax.axis_index("ckpt")
    y, core = c // 2, c % 2
    row_blocks = group // NCB
    own_rows, own_grads, own_weight = act_table[0], grads[0], weights[0, 0]
    local, depth = own_rows.shape
    tokens = token_ids.shape[1]
    features = depth // row_blocks // size

    starts = jnp.cumsum(lengths[0]) - lengths[0]
    meta = jnp.concatenate([starts, lengths[0], token_ids[0]]).astype(jnp.int32)
    metas = [meta, swap(meta, "ckpt", 1), swap(meta, "ckpt", 2), swap(meta, "ckpt", 3)]
    count = lengths.shape[1]

    parts = own_rows.reshape(local, row_blocks, size, features)
    half = 2

    def quarter(value, index):
        return lax.dynamic_index_in_dim(value, index, 2, keepdims=False)

    far = lax.dynamic_slice_in_dim(parts, (1 - y) * half, half, 2)
    far = swap(far, "ckpt", 2)
    near = lax.dynamic_slice_in_dim(parts, y * half, half, 2)
    act0, act2 = quarter(near, core), quarter(far, core)
    act1 = swap(quarter(near, 1 - core), "ckpt", 1)
    act3 = swap(quarter(far, 1 - core), "ckpt", 1)

    far_w = lax.dynamic_slice_in_dim(own_weight, (1 - y) * 2 * features, 2 * features, 0)
    far_w = swap(far_w, "ckpt", 2)

    def rows_of(value, index):
        return lax.dynamic_slice_in_dim(value, index * features, features, 0)

    weight1 = swap(rows_of(own_weight, y * 2 + 1 - core), "ckpt", 1)
    weight3 = swap(rows_of(far_w, 1 - core), "ckpt", 1)
    weight_slots = (own_weight, weight1, far_w, weight3)
    weight_rows = (c, 0, core, 0)

    width = own_grads.shape[1] // NCB
    cut = min(-(-(width // 2) // CUT) * CUT, width - LANES)
    chunks = ((0, cut), (cut, width))
    grad_slots, previous = [], None
    for low, high in chunks:
        piece = own_grads.reshape(local, NCB, width)[:, :, low:high]
        piece = jnp.transpose(piece, (1, 0, 2))
        if row_blocks > 1:
            piece = jnp.broadcast_to(piece[None], (row_blocks,) + piece.shape)
            piece = piece.reshape(group, local, high - low)
        if previous is not None:
            piece, previous = lax.optimization_barrier((piece, previous))
            grad_slots[-1][0] = previous
        grad0 = lax.all_to_all(piece, "fsdp", split_axis=0, concat_axis=0, tiled=True)
        grad0 = grad0.reshape(tokens, high - low)
        previous = grad0
        grad_slots.append([grad0, None, None, None])
    for slots in grad_slots:
        slots[2] = swap(slots[0], "ckpt", 2)
        slots[1] = swap(slots[0], "ckpt", 1)
        slots[3] = swap(slots[2], "ckpt", 1)

    ids = [m[2 * count:] for m in metas]

    def gathered(a, b, pair_ids):
        if row_blocks == 1:
            pieces = gather_line(jnp.stack([a[:, 0], b[:, 0]]))
            return permute_pair(jnp.stack(pair_ids), pieces)
        both = jnp.stack([a, b])
        both = jnp.transpose(both, (2, 0, 1, 3))[:, None]
        both = jnp.broadcast_to(both, (row_blocks, NCB, 2, local, features))
        both = both.reshape(group, 2, local, features)
        table = lax.all_to_all(both, "fsdp", split_axis=0, concat_axis=0, tiled=True)
        tables = (table[:, 0].reshape(tokens, features), table[:, 1].reshape(tokens, features))
        return jnp.stack([permuted(rows, place) for rows, place in zip(tables, pair_ids)])

    near_acts = gathered(act0, act1, ids[:2])
    far_acts = gathered(act2, act3, ids[2:])
    bounds = jnp.stack(
        [jnp.append(m[:2 * count], jnp.int32(row)) for m, row in zip(metas, weight_rows)]
    )
    plan = ((0, 1), (2, 3))
    done = None
    for index, (low, high) in enumerate(chunks):
        carry = None
        for slots in plan:
            last = slots[-1] == size - 1
            take = lambda values: [values[j] for j in slots]
            carry = add_slots(
                bounds[slots[0]:slots[-1] + 1], near_acts if slots[0] < 2 else far_acts,
                slots[0] % 2, take(grad_slots[index]), take(weight_slots), carry, done, low, last, size,
            )
        done = carry
    merged, merge_weight = done
    return merged[None], merge_weight[None]


def solution(mesh):
    placed = (
        P("ckpt", "fsdp", None),
        P("ckpt", None),
        P("ckpt", None),
        P("ckpt", "fsdp", None),
        P("ckpt", "fsdp", None, None),
    )
    return jax.shard_map(
        body,
        mesh=mesh,
        in_specs=placed,
        out_specs=(P("fsdp", "ckpt", None), P("fsdp", "ckpt", None)),
        check_vma=False,
    )
```

```python
import functools

import jax
import jax.numpy as jnp
from jax import lax
from jax.experimental import pallas as pl
from jax.experimental.pallas import tpu as pltpu
from jax.sharding import PartitionSpec as P


NCB = 8
MOST = 384
LANES = 128
COLS = (256, 128)
ROWS = 256
CUT = 512

prior_mass = 0.1


def swap(value, axis, bit):
    size = lax.axis_size(axis)
    return lax.ppermute(value, axis, [(i, i ^ bit) for i in range(size)])


def slot_kernel(slots, first, last, group_size, window, block, bounds, act, *refs):
    grads, refs = refs[:slots], refs[slots:]
    weights, refs = refs[:slots], refs[slots:]
    den, num = refs[-2:]
    outs, prev = refs[-4:-2], refs[:-4]
    (_, features, tokens), count = act.shape, (bounds.shape[1] - 1) // 2
    step = ROWS if features % ROWS == 0 else features

    def base_of(slot, example):
        base = jnp.minimum((bounds[slot, example] // LANES) * LANES, tokens - window)
        return pl.multiple_of(base, LANES)

    for slot in range(slots):
        examples = []
        for example in range(count):
            begin = bounds[slot, example]
            end = begin + bounds[slot, count + example]
            base = base_of(slot, example)
            place = base + lax.broadcasted_iota(jnp.int32, (window, block), 0)
            rows = grads[slot][pl.ds(base, window), :]
            rows = jnp.where((place >= begin) & (place < end), rows, jnp.zeros_like(rows))
            examples.append((base, rows))
        for low in range(0, features, step):
            part = pl.ds(low, step)
            total = jnp.float32(prior_mass)
            for base, rows in examples:
                mine = act[slot, part, pl.ds(base, window)]
                one = jnp.dot(mine, rows, preferred_element_type=jnp.float32)
                total = total + one * one
            weighted = total * weights[slot][part, :].astype(jnp.float32)
            if slot > 0:
                total, weighted = total + den[part, :], weighted + num[part, :]
            elif not first:
                total, weighted = total + prev[0][part, :], weighted + prev[1][part, :]
            den[part, :] = total
            num[part, :] = weighted

    if last:
        outs[0][...] = (num[...] / den[...]).astype(jnp.bfloat16)
        outs[1][...] = den[...] / group_size
    else:
        outs[0][...] = den[...]
        outs[1][...] = num[...]


def add_slots(bounds, act, at, grads, weights, prev, done, offset, last, group_size):
    slots = len(grads)
    (_, features, tokens), count = act.shape, (bounds.shape[1] - 1) // 2
    span, width = grads[0].shape[1], weights[0].shape[1]
    block = next(b for b in COLS if span % b == 0 and offset % b == 0)
    window = min(-(-(MOST + LANES - 1) // LANES) * LANES, tokens)
    first = prev is None
    skip = offset // block
    chunk = pl.BlockSpec((features, block), lambda j, b: (0, j))
    tile = pl.BlockSpec((features, block), lambda j, b: (0, j + skip))
    whole = pl.BlockSpec(
        (slots, features, tokens), lambda j, b: (at // slots, 0, 0), pipeline_mode=pl.Buffered(1)
    )
    in_specs = [whole]
    in_specs += [pl.BlockSpec((tokens, block), lambda j, b: (0, j))] * slots
    in_specs += [
        pl.BlockSpec((features, block), lambda j, b, s=s: (b[s, 2 * count], j + skip))
        for s in range(slots)
    ]
    operands = [act] + list(grads) + list(weights)
    if not first:
        in_specs += [chunk, chunk]
        operands += list(prev)
    aliases = {}
    if last:
        outs = (
            jax.ShapeDtypeStruct((features, width), jnp.bfloat16),
            jax.ShapeDtypeStruct((features, width), jnp.float32),
        )
        if done is not None:
            aliases = {len(operands) + 1: 0, len(operands) + 2: 1}
            in_specs += [pl.BlockSpec(memory_space=pl.ANY)] * 2
            operands += list(done)
    else:
        outs = (jax.ShapeDtypeStruct((features, span), jnp.float32),) * 2
    return pl.pallas_call(
        functools.partial(slot_kernel, slots, first, last, group_size, window, block),
        out_shape=outs,
        grid_spec=pltpu.PrefetchScalarGridSpec(
            num_scalar_prefetch=1,
            grid=(span // block,),
            in_specs=in_specs,
            out_specs=(tile, tile) if last else (chunk, chunk),
            scratch_shapes=[
                pltpu.VMEM((features, block), jnp.float32),
                pltpu.VMEM((features, block), jnp.float32),
            ],
        ),
        input_output_aliases=aliases,
        cost_estimate=pl.CostEstimate(
            flops=slots * 2 * count * window * features * span,
            bytes_accessed=slots * 2 * (features + span) * tokens + 18 * features * span,
            transcendentals=0,
        ),
    )(bounds, *operands)


def gather_line(own):
    size = lax.axis_size("fsdp")
    n = size // 2

    def send(value, pairs):
        return lax.ppermute(value, "fsdp", pairs)

    line = range(size)
    right, left = [own], [own]
    pair_right = [send(own, [(i, i ^ 1) for i in line])]
    pair_left = [pair_right[0]]
    for k in range(1, n):
        reach = [i for i in line if i // 2 >= k - 1 and i // 2 + 1 < n]
        right.append(send(right[-1], [(i, i + 2) for i in reach]))
        reach = [i for i in line if i // 2 < n - k + 1 and i // 2 >= 1]
        left.append(send(left[-1], [(i, i - 2) for i in reach]))
        pair_right.append(send(right[-1], [(i, i ^ 1) for i in line if i // 2 >= k]))
        pair_left.append(send(left[-1], [(i, i ^ 1) for i in line if i // 2 < n - k]))
    return right, left, pair_right, pair_left


def permute_kernel(n, where, ids, *refs):
    sources, (out, table, sems) = refs[:-3], refs[-3:]
    right, left = sources[:n], sources[n:2 * n - 1]
    pair_right, pair_left = sources[2 * n - 1:3 * n - 1], sources[3 * n - 1:]
    slot, step = pl.program_id(0), pl.program_id(1)
    z, x = where[0], where[1]

    def place(k, s):
        return lax.rem(z - k + n, n) * 2 + (x if s == 0 else 1 - x)

    def copy(source, part, k, s):
        return pltpu.make_async_copy(source.at[part], table.at[part, place(k, s)], sems.at[part, k, s])

    @pl.when((slot == 0) & (step == 0))
    def _():
        for part in range(2):
            for s, ups, downs in ((0, right, left), (1, pair_right, pair_left)):
                copy(ups[0], part, 0, s).start()
                for k in range(1, n):
                    @pl.when(z >= k)
                    def _():
                        copy(ups[k], part, k, s).start()

                    @pl.when(z < k)
                    def _():
                        copy(downs[n - k - 1], part, k, s).start()

    for part in range(2):
        @pl.when((slot == part) & (step == 0))
        def _():
            for k in range(n):
                for s in range(2):
                    copy(right[0], part, k, s).wait()

    rows = table[slot].reshape(-1, table.shape[-1])
    width = min(ROWS, ids.shape[1])
    for low in range(0, ids.shape[1], width):
        mine = ids[0, low:low + width]
        hot = lax.broadcasted_iota(jnp.int32, (width, rows.shape[0]), 1) == mine
        hot = jnp.where(hot, jnp.float32(1), jnp.float32(0)).astype(rows.dtype)
        picked = jnp.dot(hot, rows, preferred_element_type=jnp.float32).astype(rows.dtype)
        out[0, :, low:low + width] = picked.T


def permute_pair(ids, pieces):
    right, left, pair_right, pair_left = pieces
    n = len(right)
    _, local, features = right[0].shape
    tokens = ids.shape[1]
    rows = min(ROWS, tokens)
    me = lax.axis_index("fsdp")
    where = jnp.stack([me // 2, me % 2]).astype(jnp.int32)
    operands = [*right, *left[1:], *pair_right, *pair_left[1:]]
    return pl.pallas_call(
        functools.partial(permute_kernel, n),
        out_shape=jax.ShapeDtypeStruct((2, features, tokens), right[0].dtype),
        grid_spec=pltpu.PrefetchScalarGridSpec(
            num_scalar_prefetch=1,
            grid=(2, tokens // rows),
            in_specs=[pl.BlockSpec((1, rows, 1), lambda p, t, w: (p, t, 0))]
            + [pl.BlockSpec(memory_space=pl.ANY)] * len(operands),
            out_specs=pl.BlockSpec((1, features, rows), lambda p, t, w: (p, 0, t)),
            scratch_shapes=[
                pltpu.VMEM((2, 2 * n, local, features), right[0].dtype),
                pltpu.SemaphoreType.DMA((2, n, 2)),
            ],
        ),
        cost_estimate=pl.CostEstimate(
            flops=4 * tokens * tokens * features, bytes_accessed=8 * tokens * features, transcendentals=0
        ),
    )(where, ids[:, :, None], *operands)


def permuted(rows, place):
    hot = (lax.broadcasted_iota(jnp.int32, (rows.shape[0], place.shape[0]), 0) == place[None, :])
    return lax.dot_general(
        rows, hot.astype(rows.dtype), (((0,), (0,)), ((), ())), preferred_element_type=jnp.float32
    ).astype(rows.dtype)


def body(act_table, token_ids, lengths, grads, weights):
    group = lax.axis_size("fsdp")
    size = lax.axis_size("ckpt")
    c = lax.axis_index("ckpt")
    y, core = c // 2, c % 2
    row_blocks = group // NCB
    own_rows, own_grads, own_weight = act_table[0], grads[0], weights[0, 0]
    local, depth = own_rows.shape
    tokens = token_ids.shape[1]
    features = depth // row_blocks // size

    starts = jnp.cumsum(lengths[0]) - lengths[0]
    meta = jnp.concatenate([starts, lengths[0], token_ids[0]]).astype(jnp.int32)
    metas = [meta, swap(meta, "ckpt", 1), swap(meta, "ckpt", 2), swap(meta, "ckpt", 3)]
    count = lengths.shape[1]

    parts = own_rows.reshape(local, row_blocks, size, features)
    half = 2

    def quarter(value, index):
        return lax.dynamic_index_in_dim(value, index, 2, keepdims=False)

    far = lax.dynamic_slice_in_dim(parts, (1 - y) * half, half, 2)
    far = swap(far, "ckpt", 2)
    near = lax.dynamic_slice_in_dim(parts, y * half, half, 2)
    act0, act2 = quarter(near, core), quarter(far, core)
    act1 = swap(quarter(near, 1 - core), "ckpt", 1)
    act3 = swap(quarter(far, 1 - core), "ckpt", 1)

    far_w = lax.dynamic_slice_in_dim(own_weight, (1 - y) * 2 * features, 2 * features, 0)
    far_w = swap(far_w, "ckpt", 2)

    def rows_of(value, index):
        return lax.dynamic_slice_in_dim(value, index * features, features, 0)

    weight1 = swap(rows_of(own_weight, y * 2 + 1 - core), "ckpt", 1)
    weight3 = swap(rows_of(far_w, 1 - core), "ckpt", 1)
    weight_slots = (own_weight, weight1, far_w, weight3)
    weight_rows = (c, 0, core, 0)

    width = own_grads.shape[1] // NCB
    cut = min(-(-(width // 2) // CUT) * CUT, width - LANES)
    chunks = ((0, cut), (cut, width))
    grad_slots, previous = [], None
    for low, high in chunks:
        piece = own_grads.reshape(local, NCB, width)[:, :, low:high]
        piece = jnp.transpose(piece, (1, 0, 2))
        if row_blocks > 1:
            piece = jnp.broadcast_to(piece[None], (row_blocks,) + piece.shape)
            piece = piece.reshape(group, local, high - low)
        if previous is not None:
            piece, previous = lax.optimization_barrier((piece, previous))
            grad_slots[-1][0] = previous
        grad0 = lax.all_to_all(piece, "fsdp", split_axis=0, concat_axis=0, tiled=True)
        grad0 = grad0.reshape(tokens, high - low)
        previous = grad0
        grad_slots.append([grad0, None, None, None])
    for slots in grad_slots:
        slots[2] = swap(slots[0], "ckpt", 2)
        slots[1] = swap(slots[0], "ckpt", 1)
        slots[3] = swap(slots[2], "ckpt", 1)

    ids = [m[2 * count:] for m in metas]

    def gathered(a, b, pair_ids):
        if row_blocks == 1:
            pieces = gather_line(jnp.stack([a[:, 0], b[:, 0]]))
            return permute_pair(jnp.stack(pair_ids), pieces)
        both = jnp.stack([a, b])
        both = jnp.transpose(both, (2, 0, 1, 3))[:, None]
        both = jnp.broadcast_to(both, (row_blocks, NCB, 2, local, features))
        both = both.reshape(group, 2, local, features)
        table = lax.all_to_all(both, "fsdp", split_axis=0, concat_axis=0, tiled=True)
        tables = (table[:, 0].reshape(tokens, features), table[:, 1].reshape(tokens, features))
        return jnp.stack([permuted(rows, place) for rows, place in zip(tables, pair_ids)])

    near_acts = gathered(act0, act1, ids[:2])
    far_acts = gathered(act2, act3, ids[2:])
    bounds = jnp.stack(
        [jnp.append(m[:2 * count], jnp.int32(row)) for m, row in zip(metas, weight_rows)]
    )
    plans = ((0, 1), (2, 3)), ((0,), (1,), (2,), (3,))
    done = None
    for index, (low, high) in enumerate(chunks):
        carry = None
        for slots in plans[index]:
            last = slots[-1] == size - 1
            take = lambda values: [values[j] for j in slots]
            carry = add_slots(
                bounds[slots[0]:slots[-1] + 1], near_acts if slots[0] < 2 else far_acts,
                slots[0] % 2, take(grad_slots[index]), take(weight_slots), carry, done, low, last, size,
            )
        done = carry
    merged, merge_weight = done
    return merged[None], merge_weight[None]


def solution(mesh):
    placed = (
        P("ckpt", "fsdp", None),
        P("ckpt", None),
        P("ckpt", None),
        P("ckpt", "fsdp", None),
        P("ckpt", "fsdp", None, None),
    )
    return jax.shard_map(
        body,
        mesh=mesh,
        in_specs=placed,
        out_specs=(P("fsdp", "ckpt", None), P("fsdp", "ckpt", None)),
        check_vma=False,
    )
```
